32 devices in a mesh: wide: 16 (over z, y, x), narrow: 2 (over core).
Axes of the slice: x: 2, y: 2, z: 4, core: 2. Of those that a mesh axis runs over, the one named last changes fastest.
Arguments:
- pool_tokens: bfloat16 [12288, 2048], P(('wide', 'narrow')), may hold values from -6 to 6
- cotangent: bfloat16 [24576, 2048], P(('wide', 'narrow')), may hold values from -6 to 6
- slot_weights: bfloat16 [32, 3, 2048, 512], P(('wide', 'narrow')), may hold values from -6 to 6
- row_index: int32 [32, 768], P(('wide', 'narrow')), may hold values from 0 to 383
- route_weight: float32 [32, 768], P(('wide', 'narrow')), may hold values from 0.05 to 1
- slot_expert: int32 [32, 1], replicated, may hold values from 0 to 7
- next_expert: int32 [32, 1], replicated, may hold values from 0 to 7
- master: float32 [8, 3, 2048, 512], P(None, None, ('wide', 'narrow')), may hold values from -6 to 6
- moment_m: float32 [8, 3, 2048, 512], P(None, None, ('wide', 'narrow')), may hold values from -4 to 4
- moment_v: float32 [8, 3, 2048, 512], P(None, None, ('wide', 'narrow')), may hold values from 0.05 to 1
Outputs:
- token_grads: bfloat16 [12288, 2048], P(('wide', 'narrow'))
- master_next: float32 [8, 3, 2048, 512], P(None, None, ('wide', 'narrow'))
- moment_m_next: float32 [8, 3, 2048, 512], P(None, None, ('wide', 'narrow'))
- moment_v_next: float32 [8, 3, 2048, 512], P(None, None, ('wide', 'narrow'))
- next_weights: bfloat16 [32, 3, 2048, 512], P(('wide', 'narrow'))
The draws below stay inside these ranges and needn't reach their ends.
Inputs may be any that keep to these rules, and one draw needn't show every extreme that they name: `slot_expert`: every one of the 8 experts is held by at least one slot; counts are uneven. `next_expert`: every one of the 8 experts is held by at least one slot; counts are uneven. `row_index`: indices into the pool of the slot's own device; a token may appear more than once.
All inputs are finite; a program needn't handle non-finite values.
Results may differ from the reference program's by a relative error of at most 0.0065.
Values may be sent and summed in bfloat16 or wider, within the bound.
A program may use at most 128 MiB of HBM per device.

```python
import math
import jax
import jax.numpy as jnp
from jax import lax

D = 2048
H = 512
EXPERTS = 8
ROWS = 768
POOL = 384
SLOTS = 32
TOKENS = 12288
PACKED = 24576


def place_ends(result, stream_key, least, largest):
    spot = [jax.random.randint(jax.random.fold_in(stream_key, axis), (), 0, length) for axis, length in enumerate(result.shape)]
    longest = result.shape.index(max(result.shape))
    neighbour = spot[:longest] + [(spot[longest] + 1) % result.shape[longest]] + spot[longest + 1:]
    return result.at[tuple(spot)].set(least).at[tuple(neighbour)].set(largest)


def level_of(stream_key, shape, split, least, top_value):
    gain, own = 1.0, jax.random.fold_in(stream_key, 6)
    for position, shards_of in split:
        steps = jnp.exp(jax.random.uniform(jax.random.fold_in(own, position), (shards_of,), jnp.float32, least / len(split), top_value / len(split)))
        gain = gain * jnp.repeat(steps, shape[position] // shards_of).reshape([-1 if axis == position else 1 for axis in range(len(shape))])
    return gain


def different_ones(key, rows, number_of, top, lift):
    sequence = jax.random.permutation(jax.random.fold_in(key, 1), number_of)
    favour = sequence
    for power in range(3):
        favour = favour * favour // number_of
    favour = favour * lift // number_of
    chance = jax.random.randint(jax.random.fold_in(key, 2), (rows, number_of), 0, 4096) + favour
    sure = jax.random.permutation(jax.random.fold_in(key, 3), rows)[jnp.arange(number_of) % rows]
    chance = jnp.where(jnp.arange(rows)[:, None] == sure[None, :], 1 << 14, chance)
    score = chance * number_of + jnp.arange(number_of)
    return lax.top_k(score.astype(jnp.int32), top)[1].astype(jnp.int32)


def normal_values(own_key, shape, spread, bound, pieces=(), kind=jnp.bfloat16):
    drawn = spread * jax.random.normal(own_key, shape, jnp.float32)
    if pieces:
        drawn = drawn * level_of(own_key, shape, pieces, -0.22, 0.18)
    return jnp.clip(drawn, -bound, bound).astype(kind)


def setup_inputs(seed: int = 0) -> dict:
    key_list = jax.random.split(jax.random.key(seed), 11)
    return {
        "pool_tokens": normal_values(key_list[0], (TOKENS, D), 1.0, 6.0, ((0, 32),)),
        "cotangent": normal_values(key_list[1], (PACKED, D), 1.0, 6.0, ((0, 32),)),
        "slot_weights": normal_values(key_list[2], (SLOTS, 3, D, H), 1.0, 6.0, ((0, 32),)),
        "row_index": place_ends(jax.random.randint(key_list[3], (SLOTS, ROWS), 0, POOL), jax.random.fold_in(key_list[3], 1), 0, POOL - 1).astype(jnp.int32),
        "route_weight": jnp.clip(0.05 + 0.95 * jax.random.uniform(key_list[4], (SLOTS, ROWS), jnp.float32) ** level_of(key_list[4], (SLOTS, ROWS), ((0, 32),), -0.2, 0.2), 0.05, 1.0),
        "slot_expert": different_ones(key_list[5], SLOTS, EXPERTS, 1, 2048),
        "next_expert": different_ones(key_list[6], SLOTS, EXPERTS, 1, 2048),
        "master": normal_values(key_list[7], (EXPERTS, 3, D, H), 1.0, 6.0, ((2, 32),), jnp.float32),
        "moment_m": normal_values(key_list[8], (EXPERTS, 3, D, H), 0.3, 4.0, ((2, 32),), jnp.float32),
        "moment_v": jnp.clip(jnp.exp(math.log(1.0) - 2.9957323 * jax.random.uniform(key_list[9], (EXPERTS, 3, D, H), jnp.float32) ** level_of(key_list[9], (EXPERTS, 3, D, H), ((2, 32),), -0.2, 0.2)), 0.05, 1.0),
    }


def inner(left, right):
    return lax.dot_general(left, right, (((0,), (0,)), ((), ())), preferred_element_type=jnp.float32)

def against(left, right):
    return lax.dot_general(left, right, (((1,), (1,)), ((), ())), preferred_element_type=jnp.float32)

def slot_pass(rows, cotangent, weights, route):
    scale_in = weights.shape[1] ** (-0.5)
    scale_out = weights.shape[2] ** (-0.5)
    gate = jnp.dot(rows, weights[0], preferred_element_type=jnp.float32) * scale_in
    upper = jnp.dot(rows, weights[1], preferred_element_type=jnp.float32) * scale_in
    sigma = jax.nn.sigmoid(gate)
    active = gate * sigma
    hidden = (active * upper).astype(jnp.bfloat16)
    scaled = (route[:, None] * cotangent.astype(jnp.float32)).astype(jnp.bfloat16)
    back = jnp.dot(scaled, weights[2], preferred_element_type=jnp.float32) * scale_out
    d_gate = (back * upper * sigma * (1.0 + gate * (1.0 - sigma))).astype(jnp.bfloat16)
    d_up = (back * active).astype(jnp.bfloat16)
    grads = jnp.stack([inner(rows, d_gate) * scale_in, inner(rows, d_up) * scale_in, inner(scaled, hidden) * scale_out])
    inputs = (against(d_gate, weights[0]) + against(d_up, weights[1])) * scale_in
    return (grads, inputs)

def adam_step(grad, master, moment_m, moment_v):
    first = 0.9 * moment_m + 0.1 * grad
    second = 0.95 * moment_v + 0.05 * grad * grad
    fresh = master - 0.05 * (first / (jnp.sqrt(second) + 1e-08) + 0.1 * master)
    return (fresh, first, second)

def reference(pool_tokens, cotangent, slot_weights, row_index, route_weight, slot_expert, next_expert, master, moment_m, moment_v):
    pools = pool_tokens.reshape(SLOTS, POOL, D)
    cots = cotangent.reshape(SLOTS, ROWS, D)

    def visit(total, item):
        pool, cot, weights, index, route, expert = item
        rows = jnp.take(pool, index, axis=0)
        grads, inputs = slot_pass(rows, cot, weights, route)
        total = total.at[expert].add(grads)
        grad_pool = jnp.zeros((POOL, D), jnp.float32).at[index].add(inputs).astype(jnp.bfloat16)
        return (total, grad_pool)
    start = jnp.zeros((EXPERTS, 3, D, H), jnp.float32)
    total, grad_pools = lax.scan(visit, start, (pools, cots, slot_weights, row_index, route_weight, slot_expert[:, 0]))
    fresh, first, second = adam_step(total, master, moment_m, moment_v)
    next_weights = jnp.take(fresh.astype(jnp.bfloat16), next_expert[:, 0], axis=0)
    return (grad_pools.reshape(TOKENS, D), fresh, first, second, next_weights)
```

```python
import functools

import jax
import jax.numpy as jnp
from jax import lax
from jax.experimental import pallas as pl
from jax.experimental.pallas import tpu as pltpu
from jax.sharding import PartitionSpec as P

EXPERTS = 8
MESH = pl.DeviceIdType.MESH
ROW_TILE = 16
COL_TILE = 256
UNROLL = 4


def inner(left, right):
    return lax.dot_general(
        left, right, (((0,), (0,)), ((), ())), preferred_element_type=jnp.float32
    )


def against(left, right):
    return lax.dot_general(
        left, right, (((1,), (1,)), ((), ())), preferred_element_type=jnp.float32
    )


def slot_pass(pool, picked, cotangent, weights, route):
    scale_in = weights.shape[1] ** (-0.5)
    scale_out = weights.shape[2] ** (-0.5)
    tokens = jnp.arange(pool.shape[0], dtype=jnp.int32)
    spread = (picked[:, None] == tokens[None, :]).astype(jnp.bfloat16)
    rows = jnp.dot(spread, pool, preferred_element_type=jnp.float32).astype(jnp.bfloat16)
    gate = jnp.dot(rows, weights[0], preferred_element_type=jnp.float32) * scale_in
    upper = jnp.dot(rows, weights[1], preferred_element_type=jnp.float32) * scale_in
    sigma = jax.nn.sigmoid(gate)
    active = gate * sigma
    hidden = (active * upper).astype(jnp.bfloat16)
    scaled = (route[:, None] * cotangent.astype(jnp.float32)).astype(jnp.bfloat16)
    back = jnp.dot(scaled, weights[2], preferred_element_type=jnp.float32) * scale_out
    d_gate = (back * upper * sigma * (1.0 + gate * (1.0 - sigma))).astype(jnp.bfloat16)
    d_up = (back * active).astype(jnp.bfloat16)
    grads = jnp.stack(
        [
            (inner(rows, d_gate) * scale_in).astype(jnp.bfloat16),
            (inner(rows, d_up) * scale_in).astype(jnp.bfloat16),
            (inner(scaled, hidden) * scale_out).astype(jnp.bfloat16),
        ]
    )
    sum_gate = inner(spread, d_gate).astype(jnp.bfloat16)
    sum_up = inner(spread, d_up).astype(jnp.bfloat16)
    inputs = (against(sum_gate, weights[0]) + against(sum_up, weights[1])) * scale_in
    return grads, inputs.astype(jnp.bfloat16)


def drain(ref, sem):
    pltpu.make_async_copy(ref, ref, sem).wait()


def exchange(
    narrow_count,
    owners,
    nexts,
    grads,
    master,
    moment_m,
    moment_v,
    master_out,
    m_out,
    v_out,
    next_out,
    recv,
    states,
    part,
    part_in,
    fresh,
    stage,
    loc_sem,
    load_sem,
    save_sem,
    first_send,
    far_recv,
    near_recv,
    part_send,
    part_recv,
    fresh_send,
    fresh_recv,
    out_send,
    out_recv,
    out_loc,
    *fresh_far,
):
    parts, members, block, hidden_units = grads.shape
    half = members // 2
    me = lax.axis_index("wide") * narrow_count + lax.axis_index("narrow")
    group = me // half
    spot = me % half
    base = group * half
    other_base = half - base
    mirror = other_base + spot

    def device(index):
        return (index // narrow_count, index % narrow_count)

    def peer_of(step):
        return (spot + step) % half

    barrier = pltpu.get_barrier_semaphore()

    def greet(step, carry):
        pl.semaphore_signal(
            barrier, inc=1, device_id=device(base + peer_of(step)), device_id_type=MESH
        )
        return carry

    pl.semaphore_signal(barrier, inc=1, device_id=device(mirror), device_id_type=MESH)
    lax.fori_loop(1, half, greet, 0)
    pl.semaphore_wait(barrier, half)

    def send_first(k):
        for start, sem in ((other_base, far_recv), (base, near_recv)):

            def send(step, carry):
                peer = peer_of(step)
                pltpu.make_async_remote_copy(
                    src_ref=grads.at[k, start + peer],
                    dst_ref=recv.at[k, start + spot],
                    send_sem=first_send.at[k],
                    recv_sem=sem.at[k],
                    device_id=device(base + peer),
                    device_id_type=MESH,
                ).start()
                return carry

            lax.fori_loop(1, half, send, 0)

    def own_first(k):
        for start in (other_base, base):
            pltpu.make_async_copy(
                grads.at[k, start + spot], recv.at[k, start + spot], loc_sem.at[k]
            ).start()

    def loads(k):
        for i, ref in enumerate((master, moment_m, moment_v)):
            pltpu.make_async_copy(ref.at[:, k], states.at[i, k], load_sem.at[i, k]).start()

    row_tile = min(ROW_TILE, block)
    col_tile = min(COL_TILE, hidden_units)

    def tiles(body):
        def rows_of(r, carry):
            rows = pl.ds(pl.multiple_of(r * row_tile, row_tile), row_tile)

            def cols_of(c, inside):
                body(rows, pl.ds(pl.multiple_of(c * col_tile, col_tile), col_tile))
                return inside

            return lax.fori_loop(0, hidden_units // col_tile, cols_of, carry)

        lax.fori_loop(0, block // row_tile, rows_of, 0)

    def sums(k, start, rows, cols, init):
        def add(outer, totals):
            for u in range(UNROLL):
                s = outer * UNROLL + u
                value = recv[k, start + s, rows, cols].astype(jnp.float32)
                totals = tuple(
                    total + value * owners[e * members + base + s]
                    for e, total in enumerate(totals)
                )
            return totals

        return lax.fori_loop(0, half // UNROLL, add, init)

    def mirror_copy(src, dst, send, arrive):
        return pltpu.make_async_remote_copy(
            src_ref=src,
            dst_ref=dst,
            send_sem=send,
            recv_sem=arrive,
            device_id=device(mirror),
            device_id_type=MESH,
        )

    def partial(k):
        drain(recv.at[k, pl.ds(0, 2)], loc_sem.at[k])
        drain(recv.at[k, pl.ds(0, half - 1)], far_recv.at[k])

        def body(rows, cols):
            zero = jnp.zeros((row_tile, col_tile), jnp.float32)
            totals = sums(k, other_base, rows, cols, (zero,) * EXPERTS)
            for e, total in enumerate(totals):
                part[k, e, rows, cols] = total.astype(jnp.bfloat16)

        tiles(body)
        mirror_copy(part.at[k], part_in.at[k], part_send.at[k], part_recv.at[k]).start()

    def refill(k, which, owner):
        held = fresh_far[k] if which else fresh.at[k]

        def fill(step, carry):
            peer = peer_of(step)
            stage[k, which * half + peer] = held[nexts[base + peer]]
            pltpu.make_async_remote_copy(
                src_ref=stage.at[k, which * half + peer],
                dst_ref=next_out.at[k, owner],
                send_sem=out_send.at[k],
                recv_sem=out_recv.at[k],
                device_id=device(base + peer),
                device_id_type=MESH,
            ).start()
            return carry

        lax.fori_loop(1, half, fill, 0)
        stage[k, which * half + spot] = held[nexts[base + spot]]
        pltpu.make_async_copy(
            stage.at[k, which * half + spot], next_out.at[k, owner], out_loc.at[k, which]
        ).start()

    def update(k):
        for i in range(3):
            drain(states.at[i, k], load_sem.at[i, k])
        drain(recv.at[k, pl.ds(0, half - 1)], near_recv.at[k])
        drain(part_in.at[k], part_recv.at[k])

        def body(rows, cols):
            init = tuple(
                part_in[k, e, rows, cols].astype(jnp.float32) for e in range(EXPERTS)
            )
            totals = sums(k, base, rows, cols, init)
            for e, grad in enumerate(totals):
                held = states[0, k, e, rows, cols]
                first = 0.9 * states[1, k, e, rows, cols] + 0.1 * grad
                second = 0.95 * states[2, k, e, rows, cols] + 0.05 * grad * grad
                value = held - 0.05 * (first / (jnp.sqrt(second) + 1e-08) + 0.1 * held)
                states[0, k, e, rows, cols] = value
                states[1, k, e, rows, cols] = first
                states[2, k, e, rows, cols] = second
                fresh[k, e, rows, cols] = value.astype(jnp.bfloat16)

        tiles(body)
        mirror_copy(
            fresh.at[k], fresh_far[k], fresh_send.at[k], fresh_recv.at[k]
        ).start()
        refill(k, 0, me)
        for i, ref in enumerate((master_out, m_out, v_out)):
            pltpu.make_async_copy(states.at[i, k], ref.at[:, k], save_sem.at[i, k]).start()

    def relay(k):
        drain(fresh_far[k], fresh_recv.at[k])
        refill(k, 1, mirror)

    ahead = min(2, parts)
    for k in range(ahead):
        send_first(k)
        own_first(k)
    for k in range(parts):
        loads(k)
    for k in range(parts + 2):
        if k < parts:
            partial(k)
            if k + ahead < parts:
                send_first(k + ahead)
                own_first(k + ahead)
        if 1 <= k <= parts:
            update(k - 1)
        if k >= 2:
            relay(k - 2)
    for k in range(parts):
        drain(recv.at[k, pl.ds(0, 2 * (half - 1))], first_send.at[k])
        drain(part.at[k], part_send.at[k])
        drain(fresh.at[k], fresh_send.at[k])
        drain(stage.at[k, pl.ds(0, 2 * (half - 1))], out_send.at[k])
        drain(next_out.at[k, pl.ds(0, 2 * (half - 1))], out_recv.at[k])
        for which in range(2):
            drain(next_out.at[k, which], out_loc.at[k, which])
        for i in range(3):
            drain(states.at[i, k], save_sem.at[i, k])


def local(
    pool_tokens,
    cotangent,
    slot_weights,
    row_index,
    route_weight,
    slot_expert,
    next_expert,
    master,
    moment_m,
    moment_v,
):
    grads, token_grads = slot_pass(
        pool_tokens, row_index[0], cotangent, slot_weights[0], route_weight[0]
    )
    narrow_count = lax.axis_size("narrow")
    members = lax.axis_size("wide") * narrow_count
    parts, width, hidden_units = grads.shape
    block = width // members
    half = members // 2
    owners = (slot_expert[:, 0][None, :] == jnp.arange(EXPERTS, dtype=jnp.int32)[:, None]).astype(
        jnp.float32
    )
    anywhere = pl.BlockSpec(memory_space=pl.ANY)
    scalars = pl.BlockSpec(memory_space=pltpu.SMEM)
    dma = pltpu.SemaphoreType.DMA
    state = jax.ShapeDtypeStruct(master.shape, jnp.float32)
    bf16 = jnp.bfloat16
    fresh, first, second, refilled = pl.pallas_call(
        functools.partial(exchange, narrow_count),
        out_shape=(
            state,
            state,
            state,
            jax.ShapeDtypeStruct((parts, members, block, hidden_units), bf16),
        ),
        in_specs=[scalars, scalars] + [anywhere] * 4,
        out_specs=(anywhere,) * 4,
        scratch_shapes=[
            pltpu.VMEM((parts, members, block, hidden_units), bf16),
            pltpu.VMEM((3, parts, EXPERTS, block, hidden_units), jnp.float32),
            pltpu.VMEM((parts, EXPERTS, block, hidden_units), bf16),
            pltpu.VMEM((parts, EXPERTS, block, hidden_units), bf16),
            pltpu.VMEM((parts, EXPERTS, block, hidden_units), bf16),
            pltpu.VMEM((parts, 2 * half, block, hidden_units), bf16),
            dma((parts,)),
            dma((3, parts)),
            dma((3, parts)),
            dma((parts,)),
            dma((parts,)),
            dma((parts,)),
            dma((parts,)),
            dma((parts,)),
            dma((parts,)),
            dma((parts,)),
            dma((parts,)),
            dma((parts,)),
            dma((parts, 2)),
        ]
        + [pltpu.VMEM((EXPERTS, block, hidden_units), bf16)] * parts,
        compiler_params=pltpu.CompilerParams(
            collective_id=0, has_side_effects=True, vmem_limit_bytes=60 * 1024 * 1024
        ),
    )(
        owners.reshape(-1),
        next_expert[:, 0],
        grads.reshape(parts, members, block, hidden_units),
        master,
        moment_m,
        moment_v,
    )
    next_weights = refilled.reshape(1, parts, width, hidden_units)
    return (token_grads, fresh, first, second, next_weights)


def solution(mesh):
    in_specs = (
        P(("wide", "narrow"), None),
        P(("wide", "narrow"), None),
        P(("wide", "narrow"), None, None, None),
        P(("wide", "narrow"), None),
        P(("wide", "narrow"), None),
        P(),
        P(),
        P(None, None, ("wide", "narrow"), None),
        P(None, None, ("wide", "narrow"), None),
        P(None, None, ("wide", "narrow"), None),
    )
    out_specs = (
        P(("wide", "narrow"), None),
        P(None, None, ("wide", "narrow"), None),
        P(None, None, ("wide", "narrow"), None),
        P(None, None, ("wide", "narrow"), None),
        P(("wide", "narrow"), None, None, None),
    )
    return jax.shard_map(local, mesh=mesh, in_specs=in_specs, out_specs=out_specs, check_vma=False)
```

```python
import functools

import jax
import jax.numpy as jnp
from jax import lax
from jax.experimental import pallas as pl
from jax.experimental.pallas import tpu as pltpu
from jax.sharding import PartitionSpec as P

EXPERTS = 8
MESH = pl.DeviceIdType.MESH
ROW_TILE = 16
COL_TILE = 256
WIDE_TILE = 256
UNROLL = 4


def inner(left, right):
    return lax.dot_general(
        left, right, (((0,), (0,)), ((), ())), preferred_element_type=jnp.float32
    )


def against(left, right):
    return lax.dot_general(
        left, right, (((1,), (1,)), ((), ())), preferred_element_type=jnp.float32
    )


def slot_pass(pool, row_index, cotangent, weights, route):
    scale_in = weights.shape[1] ** (-0.5)
    scale_out = weights.shape[2] ** (-0.5)
    tokens = jnp.arange(pool.shape[0], dtype=jnp.int32)
    spread = (tokens[:, None] == row_index).astype(jnp.bfloat16)
    rows = inner(spread, pool).astype(jnp.bfloat16)
    gate = jnp.dot(rows, weights[0], preferred_element_type=jnp.float32) * scale_in
    upper = jnp.dot(rows, weights[1], preferred_element_type=jnp.float32) * scale_in
    sigma = jax.nn.sigmoid(gate)
    active = gate * sigma
    hidden = (active * upper).astype(jnp.bfloat16)
    scaled = (route.T * cotangent.astype(jnp.float32)).astype(jnp.bfloat16)
    back = jnp.dot(scaled, weights[2], preferred_element_type=jnp.float32) * scale_out
    d_gate = (back * upper * sigma * (1.0 + gate * (1.0 - sigma))).astype(jnp.bfloat16)
    d_up = (back * active).astype(jnp.bfloat16)
    down_grad = (inner(scaled, hidden) * scale_out).astype(jnp.bfloat16)
    return rows, d_gate, d_up, down_grad


def drain(ref, sem):
    pltpu.make_async_copy(ref, ref, sem).wait()


def exchange(
    narrow_count,
    members,
    experts_now,
    nexts,
    row_index,
    down_grad,
    rows_in,
    d_gate_in,
    d_up_in,
    weights,
    master,
    moment_m,
    moment_v,
    master_out,
    m_out,
    v_out,
    next_out,
    tokens_out,
    owners,
    made,
    rows_held,
    d_held,
    w_held,
    token_sums,
    recv,
    part,
    part_in,
    fresh,
    stage,
    in_sem,
    loc_sem,
    load_sem,
    first_send,
    far_recv,
    near_recv,
    part_send,
    part_recv,
    fresh_send,
    fresh_recv,
    out_send,
    out_recv,
    out_loc,
    *fresh_far,
):
    parts, _, block, hidden_units = recv.shape
    width = made.shape[1]
    scale_in = width ** (-0.5)
    states = (master_out, m_out, v_out)
    half = members // 2
    me = lax.axis_index("wide") * narrow_count + lax.axis_index("narrow")
    group = me // half
    spot = me % half
    base = group * half
    other_base = half - base
    mirror = other_base + spot

    def device(index):
        return (index // narrow_count, index % narrow_count)

    def peer_of(step):
        return (spot + step) % half

    barrier = pltpu.get_barrier_semaphore()

    def greet(step, carry):
        pl.semaphore_signal(
            barrier, inc=1, device_id=device(base + peer_of(step)), device_id_type=MESH
        )
        return carry

    pl.semaphore_signal(barrier, inc=1, device_id=device(mirror), device_id_type=MESH)
    lax.fori_loop(1, half, greet, 0)
    pl.semaphore_wait(barrier, half)

    def source(k, owner):
        span = pl.ds(pl.multiple_of(owner * block, block), block)
        return down_grad.at[span] if k == parts - 1 else made.at[k, span]

    def wide_tiles(body):
        tile = min(WIDE_TILE, width)

        def step(t, carry):
            body(pl.ds(pl.multiple_of(t * tile, tile), tile))
            return carry

        lax.fori_loop(0, width // tile, step, 0)

    def make(k):
        def body(span):
            product = inner(rows_held[:, span], d_held[k])
            made[k, span, :] = (product * scale_in).astype(jnp.bfloat16)

        wide_tiles(body)

    def token_grads():
        shape = (token_sums.shape[1], row_index.shape[1])
        tokens = lax.broadcasted_iota(jnp.int32, shape, 0)
        spread = jnp.where(tokens == row_index[...], 1.0, 0.0).astype(jnp.bfloat16)
        for k in range(parts - 1):
            token_sums[k] = jnp.dot(
                spread, d_held[k], preferred_element_type=jnp.float32
            ).astype(jnp.bfloat16)

        def body(span):
            total = against(token_sums[0], w_held[0, span, :])
            total = total + against(token_sums[1], w_held[1, span, :])
            tokens_out[:, span] = (total * scale_in).astype(jnp.bfloat16)

        wide_tiles(body)

    def tabulate(slot, carry):
        for e in range(EXPERTS):
            owners[e * members + slot] = jnp.where(experts_now[slot] == e, 1.0, 0.0)
        return carry

    def send_first(k):
        for start, sem in ((other_base, far_recv), (base, near_recv)):

            def send(step, carry):
                peer = peer_of(step)
                pltpu.make_async_remote_copy(
                    src_ref=source(k, start + peer),
                    dst_ref=recv.at[k, start + spot],
                    send_sem=first_send.at[k],
                    recv_sem=sem.at[k],
                    device_id=device(base + peer),
                    device_id_type=MESH,
                ).start()
                return carry

            lax.fori_loop(1, half, send, 0)

    def own_first(k):
        for start in (other_base, base):
            pltpu.make_async_copy(
                source(k, start + spot), recv.at[k, start + spot], loc_sem.at[k]
            ).start()

    def loads(k):
        for i, ref in enumerate((master, moment_m, moment_v)):
            pltpu.make_async_copy(ref.at[:, k], states[i].at[:, k], load_sem.at[i, k]).start()

    row_tile = min(ROW_TILE, block)
    col_tile = min(COL_TILE, hidden_units)

    def tiles(body):
        def rows_of(r, carry):
            rows = pl.ds(pl.multiple_of(r * row_tile, row_tile), row_tile)

            def cols_of(c, inside):
                body(rows, pl.ds(pl.multiple_of(c * col_tile, col_tile), col_tile))
                return inside

            return lax.fori_loop(0, hidden_units // col_tile, cols_of, carry)

        lax.fori_loop(0, block // row_tile, rows_of, 0)

    def sums(k, start, rows, cols, init):
        def add(outer, totals):
            for u in range(UNROLL):
                s = outer * UNROLL + u
                value = recv[k, start + s, rows, cols].astype(jnp.float32)
                totals = tuple(
                    total + value * owners[e * members + base + s]
                    for e, total in enumerate(totals)
                )
            return totals

        return lax.fori_loop(0, half // UNROLL, add, init)

    def mirror_copy(src, dst, send, arrive):
        return pltpu.make_async_remote_copy(
            src_ref=src,
            dst_ref=dst,
            send_sem=send,
            recv_sem=arrive,
            device_id=device(mirror),
            device_id_type=MESH,
        )

    def partial(k):
        drain(recv.at[k, pl.ds(0, 2)], loc_sem.at[k])
        drain(recv.at[k, pl.ds(0, half - 1)], far_recv.at[k])

        def body(rows, cols):
            zero = jnp.zeros((row_tile, col_tile), jnp.float32)
            totals = sums(k, other_base, rows, cols, (zero,) * EXPERTS)
            for e, total in enumerate(totals):
                part[k, e, rows, cols] = total.astype(jnp.bfloat16)

        tiles(body)
        mirror_copy(part.at[k], part_in.at[k], part_send.at[k], part_recv.at[k]).start()

    def refill(k, which, owner):
        held = fresh_far[k] if which else fresh.at[k]

        def fill(step, carry):
            peer = peer_of(step)
            stage[k, which * half + peer] = held[nexts[base + peer]]
            pltpu.make_async_remote_copy(
                src_ref=stage.at[k, which * half + peer],
                dst_ref=next_out.at[k, owner],
                send_sem=out_send.at[k],
                recv_sem=out_recv.at[k],
                device_id=device(base + peer),
                device_id_type=MESH,
            ).start()
            return carry

        lax.fori_loop(1, half, fill, 0)
        stage[k, which * half + spot] = held[nexts[base + spot]]
        pltpu.make_async_copy(
            stage.at[k, which * half + spot], next_out.at[k, owner], out_loc.at[k, which]
        ).start()

    def update(k):
        for i in range(3):
            drain(states[i].at[:, k], load_sem.at[i, k])
        drain(recv.at[k, pl.ds(0, half - 1)], near_recv.at[k])
        drain(part_in.at[k], part_recv.at[k])

        def body(rows, cols):
            init = tuple(
                part_in[k, e, rows, cols].astype(jnp.float32) for e in range(EXPERTS)
            )
            totals = sums(k, base, rows, cols, init)
            for e, grad in enumerate(totals):
                held = states[0][e, k, rows, cols]
                first = 0.9 * states[1][e, k, rows, cols] + 0.1 * grad
                second = 0.95 * states[2][e, k, rows, cols] + 0.05 * grad * grad
                value = held - 0.05 * (first / (jnp.sqrt(second) + 1e-08) + 0.1 * held)
                states[0][e, k, rows, cols] = value
                states[1][e, k, rows, cols] = first
                states[2][e, k, rows, cols] = second
                fresh[k, e, rows, cols] = value.astype(jnp.bfloat16)

        tiles(body)
        mirror_copy(
            fresh.at[k], fresh_far[k], fresh_send.at[k], fresh_recv.at[k]
        ).start()
        refill(k, 0, me)

    def relay(k):
        drain(fresh_far[k], fresh_recv.at[k])
        refill(k, 1, mirror)

    order = (parts - 1,) + tuple(range(parts - 1))
    send_first(order[0])
    own_first(order[0])
    inputs = (
        (rows_in, rows_held),
        (d_gate_in, d_held.at[0]),
        (d_up_in, d_held.at[1]),
        (weights.at[0, pl.ds(0, 2)], w_held),
    )
    for i, (src, dst) in enumerate(inputs):
        pltpu.make_async_copy(src, dst, in_sem.at[i]).start()
    for k in order:
        loads(k)
    for i, (src, dst) in enumerate(inputs):
        pltpu.make_async_copy(src, dst, in_sem.at[i]).wait()
    make(order[1])
    send_first(order[1])
    own_first(order[1])
    for k in order[2:]:
        make(k)
    lax.fori_loop(0, members, tabulate, 0)
    token_grads()
    for step in range(parts + 2):
        if step < parts:
            partial(order[step])
            if step + 2 < parts:
                send_first(order[step + 2])
                own_first(order[step + 2])
        if 1 <= step <= parts:
            update(order[step - 1])
        if step >= 2:
            relay(order[step - 2])
    for k in range(parts):
        drain(recv.at[k, pl.ds(0, 2 * (half - 1))], first_send.at[k])
        drain(part.at[k], part_send.at[k])
        drain(fresh.at[k], fresh_send.at[k])
        drain(stage.at[k, pl.ds(0, 2 * (half - 1))], out_send.at[k])
        drain(next_out.at[k, pl.ds(0, 2 * (half - 1))], out_recv.at[k])
        for which in range(2):
            drain(next_out.at[k, which], out_loc.at[k, which])


def local(
    pool_tokens,
    cotangent,
    slot_weights,
    row_index,
    route_weight,
    slot_expert,
    next_expert,
    master,
    moment_m,
    moment_v,
):
    rows, d_gate, d_up, down_grad = slot_pass(
        pool_tokens, row_index, cotangent, slot_weights[0], route_weight
    )
    narrow_count = lax.axis_size("narrow")
    members = lax.axis_size("wide") * narrow_count
    parts, width, hidden_units = slot_weights.shape[1:]
    block = width // members
    half = members // 2
    anywhere = pl.BlockSpec(memory_space=pl.ANY)
    scalars = pl.BlockSpec(memory_space=pltpu.SMEM)
    dma = pltpu.SemaphoreType.DMA
    bf16 = jnp.bfloat16
    state = pltpu.VMEM(master.shape, jnp.float32)
    held = pl.BlockSpec(memory_space=pltpu.VMEM)
    fresh, first, second, refilled, token_grads = pl.pallas_call(
        functools.partial(exchange, narrow_count, members),
        out_shape=(
            state,
            state,
            state,
            pltpu.VMEM((parts, members, block, hidden_units), bf16),
            pltpu.VMEM(pool_tokens.shape, bf16),
        ),
        in_specs=[scalars, scalars, held] + [anywhere] * 8,
        out_specs=(held,) * 5,
        scratch_shapes=[
            pltpu.SMEM((EXPERTS * members,), jnp.float32),
            pltpu.VMEM((parts - 1, width, hidden_units), bf16),
            pltpu.VMEM(rows.shape, bf16),
            pltpu.VMEM((2,) + d_gate.shape, bf16),
            pltpu.VMEM((2, width, hidden_units), bf16),
            pltpu.VMEM((2, pool_tokens.shape[0], hidden_units), bf16),
            pltpu.VMEM((parts, members, block, hidden_units), bf16),
            pltpu.VMEM((parts, EXPERTS, block, hidden_units), bf16),
            pltpu.VMEM((parts, EXPERTS, block, hidden_units), bf16),
            pltpu.VMEM((parts, EXPERTS, block, hidden_units), bf16),
            pltpu.VMEM((parts, 2 * half, block, hidden_units), bf16),
            dma((4,)),
            dma((parts,)),
            dma((3, parts)),
            dma((parts,)),
            dma((parts,)),
            dma((parts,)),
            dma((parts,)),
            dma((parts,)),
            dma((parts,)),
            dma((parts,)),
            dma((parts,)),
            dma((parts,)),
            dma((parts, 2)),
        ]
        + [pltpu.VMEM((EXPERTS, block, hidden_units), bf16)] * parts,
        compiler_params=pltpu.CompilerParams(
            collective_id=0, has_side_effects=True, vmem_limit_bytes=42 * 1024 * 1024
        ),
    )(
        slot_expert[:, 0],
        next_expert[:, 0],
        row_index,
        down_grad,
        rows,
        d_gate,
        d_up,
        slot_weights,
        master,
        moment_m,
        moment_v,
    )
    next_weights = refilled.reshape(1, parts, width, hidden_units)
    return (token_grads, fresh, first, second, next_weights)


def solution(mesh):
    in_specs = (
        P(("wide", "narrow"), None),
        P(("wide", "narrow"), None),
        P(("wide", "narrow"), None, None, None),
        P(("wide", "narrow"), None),
        P(("wide", "narrow"), None),
        P(),
        P(),
        P(None, None, ("wide", "narrow"), None),
        P(None, None, ("wide", "narrow"), None),
        P(None, None, ("wide", "narrow"), None),
    )
    out_specs = (
        P(("wide", "narrow"), None),
        P(None, None, ("wide", "narrow"), None),
        P(None, None, ("wide", "narrow"), None),
        P(None, None, ("wide", "narrow"), None),
        P(("wide", "narrow"), None, None, None),
    )
    return jax.shard_map(local, mesh=mesh, in_specs=in_specs, out_specs=out_specs, check_vma=False)
```

```python
import functools

import jax
import jax.numpy as jnp
from jax import lax
from jax.experimental import pallas as pl
from jax.experimental.pallas import tpu as pltpu
from jax.sharding import PartitionSpec as P

EXPERTS = 8
MESH = pl.DeviceIdType.MESH
ROW_TILE = 16
COL_TILE = 256
WIDE_TILE = 256
LONG_TILE = 256
UNROLL = 4


def inner(left, right):
    return lax.dot_general(
        left, right, (((0,), (0,)), ((), ())), preferred_element_type=jnp.float32
    )


def against(left, right):
    return lax.dot_general(
        left, right, (((1,), (1,)), ((), ())), preferred_element_type=jnp.float32
    )


def drain(ref, sem):
    pltpu.make_async_copy(ref, ref, sem).wait()


def exchange(
    narrow_count,
    members,
    experts_now,
    nexts,
    row_index,
    route,
    pool,
    cotangent,
    weights,
    master,
    moment_m,
    moment_v,
    master_out,
    m_out,
    v_out,
    next_out,
    tokens_out,
    owners,
    made,
    rows_held,
    cot_held,
    spread,
    route_column,
    gates,
    hidden,
    d_held,
    w_held,
    token_sums,
    recv,
    part,
    part_in,
    fresh,
    in_sem,
    loc_sem,
    load_sem,
    first_send,
    far_recv,
    near_recv,
    part_send,
    part_recv,
    fresh_send,
    fresh_recv,
    out_send,
    out_recv,
    out_loc,
    *fresh_far,
):
    parts, _, block, hidden_units = recv.shape
    width = made.shape[1]
    scale_in = width ** (-0.5)
    scale_out = hidden_units ** (-0.5)
    states = (master_out, m_out, v_out)
    half = members // 2
    me = lax.axis_index("wide") * narrow_count + lax.axis_index("narrow")
    group = me // half
    spot = me % half
    base = group * half
    other_base = half - base
    mirror = other_base + spot

    def device(index):
        return (index // narrow_count, index % narrow_count)

    def peer_of(step):
        return (spot + step) % half

    barrier = pltpu.get_barrier_semaphore()

    def greet(step, carry):
        pl.semaphore_signal(
            barrier, inc=1, device_id=device(base + peer_of(step)), device_id_type=MESH
        )
        return carry

    pl.semaphore_signal(barrier, inc=1, device_id=device(mirror), device_id_type=MESH)
    lax.fori_loop(1, half, greet, 0)
    def source(k, owner):
        span = pl.ds(pl.multiple_of(owner * block, block), block)
        return made.at[k, span]

    def wide_tiles(body):
        tile = min(WIDE_TILE, width)

        def step(t, carry):
            body(pl.ds(pl.multiple_of(t * tile, tile), tile))
            return carry

        lax.fori_loop(0, width // tile, step, 0)

    def make(k):
        def body(span):
            if k == parts - 1:
                product = inner(cot_held[:, span], hidden[...]) * scale_out
            else:
                product = inner(rows_held[:, span], d_held[k]) * scale_in
            made[k, span, :] = product.astype(jnp.bfloat16)

        wide_tiles(body)

    def long_tiles(body):
        length = rows_held.shape[0]
        tile = min(LONG_TILE, length)

        def step(t, carry):
            body(pl.ds(pl.multiple_of(t * tile, tile), tile))
            return carry

        lax.fori_loop(0, length // tile, step, 0)

    def product_of(left, right):
        return jnp.dot(left, right, preferred_element_type=jnp.float32)

    def pick_rows():
        tokens = lax.broadcasted_iota(jnp.int32, spread.shape, 0)
        spread[...] = jnp.where(tokens == row_index[...], 1.0, 0.0).astype(jnp.bfloat16)
        length = rows_held.shape[0]
        route_column[...] = jnp.transpose(jnp.broadcast_to(route[...], (128, length)))

    def gather(span):
        rows_held[:, span] = inner(spread[...], tokens_out[:, span]).astype(jnp.bfloat16)

    def forward(span):
        rows = rows_held[span, :]
        gate = product_of(rows, w_held[0]) * scale_in
        upper = product_of(rows, w_held[1]) * scale_in
        gates[0, span, :] = gate
        gates[1, span, :] = upper
        hidden[span, :] = (gate * jax.nn.sigmoid(gate) * upper).astype(jnp.bfloat16)

    def scale_rows(span):
        column = route_column[span, pl.ds(0, 1)]
        cot_held[span, :] = (column * cot_held[span, :].astype(jnp.float32)).astype(jnp.bfloat16)

    def backward(span):
        back = product_of(cot_held[span, :], w_held[2]) * scale_out
        gate = gates[0, span, :]
        upper = gates[1, span, :]
        sigma = jax.nn.sigmoid(gate)
        slope = sigma * (1.0 + gate * (1.0 - sigma))
        d_held[0, span, :] = (back * upper * slope).astype(jnp.bfloat16)
        d_held[1, span, :] = (back * (gate * sigma)).astype(jnp.bfloat16)

    def token_grads():
        for k in range(parts - 1):
            token_sums[k] = jnp.dot(
                spread[...], d_held[k], preferred_element_type=jnp.float32
            ).astype(jnp.bfloat16)

        def body(span):
            total = against(token_sums[0], w_held[0, span, :])
            total = total + against(token_sums[1], w_held[1, span, :])
            tokens_out[:, span] = (total * scale_in).astype(jnp.bfloat16)

        wide_tiles(body)

    def tabulate(slot, carry):
        for e in range(EXPERTS):
            owners[e * members + slot] = jnp.where(experts_now[slot] == e, 1.0, 0.0)
        return carry

    def send_first(k):
        for start, sem in ((other_base, far_recv), (base, near_recv)):

            def send(step, carry):
                peer = peer_of(step)
                pltpu.make_async_remote_copy(
                    src_ref=source(k, start + peer),
                    dst_ref=recv.at[k, start + spot],
                    send_sem=first_send.at[k],
                    recv_sem=sem.at[k],
                    device_id=device(base + peer),
                    device_id_type=MESH,
                ).start()
                return carry

            lax.fori_loop(1, half, send, 0)

    def own_first(k):
        for start in (other_base, base):
            pltpu.make_async_copy(
                source(k, start + spot), recv.at[k, start + spot], loc_sem.at[k]
            ).start()

    def loads(k):
        for i, ref in enumerate((master, moment_m, moment_v)):
            pltpu.make_async_copy(ref.at[:, k], states[i].at[:, k], load_sem.at[i, k]).start()

    row_tile = min(ROW_TILE, block)
    col_tile = min(COL_TILE, hidden_units)

    def tiles(body):
        def rows_of(r, carry):
            rows = pl.ds(pl.multiple_of(r * row_tile, row_tile), row_tile)

            def cols_of(c, inside):
                body(rows, pl.ds(pl.multiple_of(c * col_tile, col_tile), col_tile))
                return inside

            return lax.fori_loop(0, hidden_units // col_tile, cols_of, carry)

        lax.fori_loop(0, block // row_tile, rows_of, 0)

    def sums(k, start, rows, cols, init):
        def add(outer, totals):
            for u in range(UNROLL):
                s = outer * UNROLL + u
                value = recv[k, start + s, rows, cols].astype(jnp.float32)
                totals = tuple(
                    total + value * owners[e * members + base + s]
                    for e, total in enumerate(totals)
                )
            return totals

        return lax.fori_loop(0, half // UNROLL, add, init)

    def mirror_copy(src, dst, send, arrive):
        return pltpu.make_async_remote_copy(
            src_ref=src,
            dst_ref=dst,
            send_sem=send,
            recv_sem=arrive,
            device_id=device(mirror),
            device_id_type=MESH,
        )

    def partial(k):
        drain(recv.at[k, pl.ds(0, 2)], loc_sem.at[k])
        drain(recv.at[k, pl.ds(0, half - 1)], far_recv.at[k])

        def body(rows, cols):
            zero = jnp.zeros((row_tile, col_tile), jnp.float32)
            totals = sums(k, other_base, rows, cols, (zero,) * EXPERTS)
            for e, total in enumerate(totals):
                part[k, e, rows, cols] = total.astype(jnp.bfloat16)

        tiles(body)
        mirror_copy(part.at[k], part_in.at[k], part_send.at[k], part_recv.at[k]).start()

    def refill(k, which, owner):
        held = fresh_far[k] if which else fresh.at[k]

        def fill(step, carry):
            peer = peer_of(step)
            recv[k, which * half + peer] = held[nexts[base + peer]]
            pltpu.make_async_remote_copy(
                src_ref=recv.at[k, which * half + peer],
                dst_ref=next_out.at[k, owner],
                send_sem=out_send.at[k],
                recv_sem=out_recv.at[k],
                device_id=device(base + peer),
                device_id_type=MESH,
            ).start()
            return carry

        lax.fori_loop(1, half, fill, 0)
        recv[k, which * half + spot] = held[nexts[base + spot]]
        pltpu.make_async_copy(
            recv.at[k, which * half + spot], next_out.at[k, owner], out_loc.at[k, which]
        ).start()

    def update(k):
        for i in range(3):
            drain(states[i].at[:, k], load_sem.at[i, k])
        drain(recv.at[k, pl.ds(0, half - 1)], near_recv.at[k])
        drain(part_in.at[k], part_recv.at[k])

        def body(rows, cols):
            init = tuple(
                part_in[k, e, rows, cols].astype(jnp.float32) for e in range(EXPERTS)
            )
            totals = sums(k, base, rows, cols, init)
            for e, grad in enumerate(totals):
                held = states[0][e, k, rows, cols]
                first = 0.9 * states[1][e, k, rows, cols] + 0.1 * grad
                second = 0.95 * states[2][e, k, rows, cols] + 0.05 * grad * grad
                value = held - 0.05 * (first / (jnp.sqrt(second) + 1e-08) + 0.1 * held)
                states[0][e, k, rows, cols] = value
                states[1][e, k, rows, cols] = first
                states[2][e, k, rows, cols] = second
                fresh[k, e, rows, cols] = value.astype(jnp.bfloat16)

        tiles(body)
        mirror_copy(
            fresh.at[k], fresh_far[k], fresh_send.at[k], fresh_recv.at[k]
        ).start()
        refill(k, 0, me)

    def relay(k):
        drain(fresh_far[k], fresh_recv.at[k])
        refill(k, 1, mirror)

    order = (parts - 1,) + tuple(range(parts - 1))
    inputs = ((pool, tokens_out), (weights.at[0], w_held), (cotangent, cot_held))
    arrivals = [
        pltpu.make_async_copy(src, dst, in_sem.at[i]) for i, (src, dst) in enumerate(inputs)
    ]
    for arrival in arrivals:
        arrival.start()
    pick_rows()
    arrivals[0].wait()
    wide_tiles(gather)
    arrivals[1].wait()
    long_tiles(forward)
    arrivals[2].wait()
    long_tiles(scale_rows)
    make(order[0])
    pl.semaphore_wait(barrier, half)
    send_first(order[0])
    own_first(order[0])
    for k in order:
        loads(k)
    long_tiles(backward)
    make(order[1])
    send_first(order[1])
    own_first(order[1])
    for k in order[2:]:
        make(k)
    lax.fori_loop(0, members, tabulate, 0)
    token_grads()
    for step in range(parts + 2):
        if step < parts:
            partial(order[step])
            if step + 2 < parts:
                send_first(order[step + 2])
                own_first(order[step + 2])
        if 1 <= step <= parts:
            update(order[step - 1])
        if step >= 2:
            relay(order[step - 2])
    for k in range(parts):
        drain(recv.at[k, pl.ds(0, 2 * (half - 1))], first_send.at[k])
        drain(part.at[k], part_send.at[k])
        drain(fresh.at[k], fresh_send.at[k])
        drain(recv.at[k, pl.ds(0, 2 * (half - 1))], out_send.at[k])
        drain(next_out.at[k, pl.ds(0, 2 * (half - 1))], out_recv.at[k])
        for which in range(2):
            drain(next_out.at[k, which], out_loc.at[k, which])


def local(
    pool_tokens,
    cotangent,
    slot_weights,
    row_index,
    route_weight,
    slot_expert,
    next_expert,
    master,
    moment_m,
    moment_v,
):
    narrow_count = lax.axis_size("narrow")
    members = lax.axis_size("wide") * narrow_count
    parts, width, hidden_units = slot_weights.shape[1:]
    block = width // members
    length = row_index.shape[1]
    pool_count = pool_tokens.shape[0]
    anywhere = pl.BlockSpec(memory_space=pl.ANY)
    scalars = pl.BlockSpec(memory_space=pltpu.SMEM)
    dma = pltpu.SemaphoreType.DMA
    bf16 = jnp.bfloat16
    state = pltpu.VMEM(master.shape, jnp.float32)
    held = pl.BlockSpec(memory_space=pltpu.VMEM)
    fresh, first, second, refilled, token_grads = pl.pallas_call(
        functools.partial(exchange, narrow_count, members),
        out_shape=(
            state,
            state,
            state,
            pltpu.VMEM((parts, members, block, hidden_units), bf16),
            pltpu.VMEM(pool_tokens.shape, bf16),
        ),
        in_specs=[scalars, scalars, held, held] + [anywhere] * 6,
        out_specs=(held,) * 5,
        scratch_shapes=[
            pltpu.SMEM((EXPERTS * members,), jnp.float32),
            pltpu.VMEM((parts, width, hidden_units), bf16),
            pltpu.VMEM((length, width), bf16),
            pltpu.VMEM((length, width), bf16),
            pltpu.VMEM((pool_count, length), bf16),
            pltpu.VMEM((length, 128), jnp.float32),
            pltpu.VMEM((2, length, hidden_units), jnp.float32),
            pltpu.VMEM((length, hidden_units), bf16),
            pltpu.VMEM((2, length, hidden_units), bf16),
            pltpu.VMEM((parts, width, hidden_units), bf16),
            pltpu.VMEM((2, pool_count, hidden_units), bf16),
            pltpu.VMEM((parts, members, block, hidden_units), bf16),
            pltpu.VMEM((parts, EXPERTS, block, hidden_units), bf16),
            pltpu.VMEM((parts, EXPERTS, block, hidden_units), bf16),
            pltpu.VMEM((parts, EXPERTS, block, hidden_units), bf16),
            dma((3,)),
            dma((parts,)),
            dma((3, parts)),
            dma((parts,)),
            dma((parts,)),
            dma((parts,)),
            dma((parts,)),
            dma((parts,)),
            dma((parts,)),
            dma((parts,)),
            dma((parts,)),
            dma((parts,)),
            dma((parts, 2)),
        ]
        + [pltpu.VMEM((EXPERTS, block, hidden_units), bf16)] * parts,
        compiler_params=pltpu.CompilerParams(
            collective_id=0, has_side_effects=True, vmem_limit_bytes=46 * 1024 * 1024
        ),
    )(
        slot_expert[:, 0],
        next_expert[:, 0],
        row_index,
        route_weight,
        pool_tokens,
        cotangent,
        slot_weights,
        master,
        moment_m,
        moment_v,
    )
    next_weights = refilled.reshape(1, parts, width, hidden_units)
    return (token_grads, fresh, first, second, next_weights)


def solution(mesh):
    in_specs = (
        P(("wide", "narrow"), None),
        P(("wide", "narrow"), None),
        P(("wide", "narrow"), None, None, None),
        P(("wide", "narrow"), None),
        P(("wide", "narrow"), None),
        P(),
        P(),
        P(None, None, ("wide", "narrow"), None),
        P(None, None, ("wide", "narrow"), None),
        P(None, None, ("wide", "narrow"), None),
    )
    out_specs = (
        P(("wide", "narrow"), None),
        P(None, None, ("wide", "narrow"), None),
        P(None, None, ("wide", "narrow"), None),
        P(None, None, ("wide", "narrow"), None),
        P(("wide", "narrow"), None, None, None),
    )
    return jax.shard_map(local, mesh=mesh, in_specs=in_specs, out_specs=out_specs, check_vma=False)
```
